32 devices in a mesh: band: 8 (over z, y), lev: 4 (over x, core).
Axes of the slice: x: 2, y: 2, z: 4, core: 2. Of those that a mesh axis runs over, the one named last changes fastest.
Arguments:
- grid_adjoint: float32 [1024, 64, 2048], P('band', 'lev'), may hold values from -6 to 6
- trajectory: float32 [1024, 64, 2048], P('band', 'lev'), may hold values from -3 to 3
- legendre_north: float32 [512, 512, 512], P(('band', 'lev')), may hold values from -0.25 to 0.25
- slot_wavenumber: int32 [512], replicated, may hold values from 0 to 511, each once
- spectral_state: float32 [512, 512, 2, 64], P(('band', 'lev')), may hold values from -6 to 6
- to_modes: float32 [64, 64], replicated, may hold values from -0.75 to 0.75
- from_modes: float32 [64, 64], replicated, may hold values from -0.75 to 0.75
- rates: float32 [64], replicated, may hold values from 0.1 to 10
Outputs:
- spectral_out: float32 [512, 512, 2, 64], P(('band', 'lev'))
- grid_out: float32 [1024, 64, 2048], P('band', 'lev')
The draws below stay inside these ranges and needn't reach their ends.
Inputs may be any that keep to these rules, and one draw needn't show every extreme that they name: `slot_wavenumber`: each wavenumber stands in exactly one slot.
All inputs are finite; a program needn't handle non-finite values.
Results may differ from the reference program's by a relative error of at most 0.000067.
Values sent between devices are 32-bit elements; how exact they have to be, the bound alone decides.
A program may use at most 192 MiB of HBM per device.

```python
import math
import jax
import jax.numpy as jnp
from jax import lax

M = 512
LAT = 1024
LON = 2048
L = 64
LH = 512


def level_of(key, dims, shards, low, largest):
    factor_of = 1.0
    for axis_at, blocks in shards:
        draws = jax.random.uniform(jax.random.fold_in(jax.random.fold_in(key, 6), axis_at), (blocks,), jnp.float32, low / len(shards), largest / len(shards))
        factor_of = factor_of * jnp.repeat(jnp.exp(draws), dims[axis_at] // blocks).reshape((-1,) + (1,) * (len(dims) - 1 - axis_at))
    return factor_of


def scatter_about(rng, dims, deviation, reach, split=(), kind=jnp.bfloat16):
    entries = jax.random.normal(rng, dims, jnp.float32) * deviation
    if len(split) > 0:
        entries = level_of(rng, dims, split, -0.22, 0.18) * entries
    return jnp.clip(entries, min=-reach, max=reach).astype(kind)


def setup_inputs(seed: int = 0) -> dict:
    key_of = jax.random.split(jax.random.key(seed), 9)
    grid_adjoint = scatter_about(key_of[0], (LAT, L, LON), 1.0, 6.0, ((0, 8), (1, 4)), jnp.float32)
    trajectory = scatter_about(key_of[1], (LAT, L, LON), 0.5, 3.0, ((0, 8), (1, 4)), jnp.float32)
    legendre_north = scatter_about(key_of[2], (M, M, LH), LH ** -0.5, 0.25, ((0, 32),), jnp.float32)
    slot_wavenumber = jax.random.permutation(key_of[3], M).astype(jnp.int32)
    spectral_state = scatter_about(key_of[4], (M, M, 2, L), 1.0, 6.0, ((0, 32),), jnp.float32)
    to_modes = scatter_about(key_of[5], (L, L), L ** -0.5, 0.75, (), jnp.float32)
    from_modes = scatter_about(key_of[6], (L, L), L ** -0.5, 0.75, (), jnp.float32)
    rates = jnp.clip(jnp.exp(jax.random.uniform(key_of[7], (L,), jnp.float32, math.log(0.1), math.log(10.0))), 0.1, 10.0)
    return dict(grid_adjoint=grid_adjoint, trajectory=trajectory, legendre_north=legendre_north, slot_wavenumber=slot_wavenumber, spectral_state=spectral_state, to_modes=to_modes, from_modes=from_modes, rates=rates)


def wave_table():
    column = jnp.arange(LON, dtype=jnp.int32)
    number = jnp.arange(M, dtype=jnp.int32)
    phase = (column[:, None] * number[None, :]) % LON
    angles = phase.astype(jnp.float32) * (2.0 * jnp.pi / LON)
    scale = jnp.float32(LON) ** -0.5
    return jnp.concatenate([jnp.cos(angles), -jnp.sin(angles)], axis=1) * scale


def unfold(north):
    depth = north.shape[0]
    parity = jnp.where(jnp.arange(depth) % 2 == 0, 1.0, -1.0).astype(jnp.float32)
    return jnp.concatenate([north, parity[:, None] * north[:, ::-1]], axis=1)


def reference(grid_adjoint, trajectory, legendre_north, slot_wavenumber, spectral_state, to_modes, from_modes, rates):
    highest = lax.Precision.HIGHEST
    table = wave_table()
    forced = grid_adjoint * (1.0 + trajectory)
    fourier = jnp.dot(forced.reshape(LAT * L, LON), table, precision=highest, preferred_element_type=jnp.float32)
    fourier = fourier.reshape(LAT, L, 2, M)
    slotted = jnp.take(fourier, slot_wavenumber, axis=3)
    columns = jnp.transpose(slotted, (3, 0, 1, 2))

    def analyse(pair):
        north, column_data = pair
        whole = unfold(north)
        return jnp.einsum('kt,tlc->kcl', whole, column_data, precision=highest)

    analysed = lax.map(analyse, (legendre_north, columns))
    depth_index = jnp.arange(M, dtype=jnp.int32)
    valid = (depth_index[None, :] < M - slot_wavenumber[:, None]).astype(jnp.float32)
    total = (analysed + spectral_state) * valid[:, :, None, None]
    degree = (slot_wavenumber[:, None] + depth_index[None, :]).astype(jnp.float32)
    helm = degree * (degree + 1.0) / (M * (M - 1.0))
    modes = jnp.einsum('skcl,pl->skcp', total, to_modes, precision=highest)
    scaled = modes / (1.0 + helm[:, :, None, None] * rates)
    spectral_out = jnp.einsum('skcp,lp->skcl', scaled, from_modes, precision=highest)

    def synthesise(pair):
        north, coeffs = pair
        whole = unfold(north)
        return jnp.einsum('kt,kcl->tlc', whole, coeffs, precision=highest)

    synthesised = lax.map(synthesise, (legendre_north, spectral_out))
    inverse = jnp.zeros((M,), jnp.int32).at[slot_wavenumber].set(jnp.arange(M, dtype=jnp.int32))
    ordered = jnp.transpose(jnp.take(synthesised, inverse, axis=0), (1, 2, 3, 0))
    grid_out = jnp.dot(ordered.reshape(LAT * L, 2 * M), table.T, precision=highest, preferred_element_type=jnp.float32)
    return spectral_out, grid_out.reshape(LAT, L, LON)
```

```python
import jax
import jax.numpy as jnp
from jax import lax
from jax.sharding import PartitionSpec as P

PRECISION = lax.Precision.HIGH


def angle_parts(steps, waves, longitudes):
    phase = waves[:, None] * steps[None, :] % longitudes
    angles = phase.astype(jnp.float32) * (2.0 * jnp.pi / longitudes)
    return jnp.cos(angles), jnp.sin(angles)


def wave_rows(longitudes, waves, devices):
    fine = min(128, longitudes)
    coarse = longitudes // fine
    scale = jnp.float32(longitudes) ** (-0.5)
    cos_a, sin_a = angle_parts(jnp.arange(coarse, dtype=jnp.int32) * fine, waves, longitudes)
    cos_b, sin_b = angle_parts(jnp.arange(fine, dtype=jnp.int32), waves, longitudes)
    cos_a, sin_a, cos_b, sin_b = lax.optimization_barrier(
        (cos_a * scale, sin_a * scale, cos_b, sin_b)
    )
    cos_at = [cos_a[:, i : i + 1] * cos_b - sin_a[:, i : i + 1] * sin_b for i in range(coarse)]
    sin_at = [-sin_a[:, i : i + 1] * cos_b - cos_a[:, i : i + 1] * sin_b for i in range(coarse)]
    cosine = jnp.concatenate(cos_at, axis=1).reshape(devices, -1, longitudes)
    negsine = jnp.concatenate(sin_at, axis=1).reshape(devices, -1, longitudes)
    return jnp.stack([cosine, negsine], axis=1).reshape(-1, longitudes)


def exchange(data):
    return lax.all_to_all(data, ("band", "lev"), split_axis=0, concat_axis=0, tiled=True)


def shards(
    grid_adjoint,
    trajectory,
    legendre_north,
    slot_wavenumber,
    spectral_state,
    to_modes,
    from_modes,
    rates,
):
    lats, levels, longitudes = grid_adjoint.shape
    slots, depth, half = legendre_north.shape
    bands = lax.axis_size("band")
    parts = lax.axis_size("lev")
    devices = bands * parts
    every = parts * levels
    me = lax.axis_index("band") * parts + lax.axis_index("lev")
    own_waves = lax.dynamic_slice_in_dim(slot_wavenumber, me * slots, slots)
    table = wave_rows(longitudes, slot_wavenumber, devices)
    even_k = jnp.arange(depth, dtype=jnp.int32) % 2 == 0

    forced = grid_adjoint * (1.0 + trajectory)
    rows = jnp.swapaxes(forced, 0, 1).reshape(levels * lats, longitudes)
    fourier = lax.dot_general(
        table, rows, (((1,), (1,)), ((), ())), precision=PRECISION, preferred_element_type=jnp.float32
    )
    arrived = exchange(fourier.reshape(devices, 2 * slots, levels * lats))
    arrived = arrived.reshape(bands, parts, 2, slots, levels, lats)
    arrived = arrived.transpose(3, 2, 1, 4, 0, 5).reshape(slots, 2 * every, bands * lats)
    north = arrived[:, :, :half]
    south = arrived[:, :, half:][:, :, ::-1]
    folded = jnp.concatenate([north + south, north - south], axis=1)
    both = lax.dot_general(
        folded, legendre_north, (((2,), (2,)), ((0,), (0,))), precision=PRECISION,
        preferred_element_type=jnp.float32,
    )
    analysed = jnp.where(even_k, both[:, : 2 * every], both[:, 2 * every :])
    analysed = analysed.reshape(slots, 2, every, depth)

    state = spectral_state.transpose(0, 2, 3, 1)
    depth_index = jnp.arange(depth, dtype=jnp.int32)
    valid = (depth_index[None, :] < depth - own_waves[:, None]).astype(jnp.float32)
    total = (analysed + state) * valid[:, None, None, :]
    degree = (own_waves[:, None] + depth_index[None, :]).astype(jnp.float32)
    helm = degree * (degree + 1.0) / (depth * (depth - 1.0))
    modes = jnp.einsum("sclk,pl->scpk", total, to_modes, precision=PRECISION)
    scaled = modes / (1.0 + helm[:, None, None, :] * rates[None, None, :, None])
    spectral = jnp.einsum("scpk,lp->sclk", scaled, from_modes, precision=PRECISION)

    coeffs = spectral.reshape(slots, 2 * every, depth)
    split = jnp.concatenate(
        [jnp.where(even_k, coeffs, 0.0), jnp.where(even_k, 0.0, coeffs)], axis=1
    )
    halves = lax.dot_general(
        split, legendre_north, (((2,), (1,)), ((0,), (0,))), precision=PRECISION,
        preferred_element_type=jnp.float32,
    )
    first = halves[:, : 2 * every]
    second = halves[:, 2 * every :]
    whole = jnp.concatenate([first + second, (first - second)[:, :, ::-1]], axis=2)
    whole = whole.reshape(slots, 2, parts, levels, bands, lats).transpose(4, 2, 1, 0, 3, 5)
    returned = exchange(whole.reshape(devices, 2 * slots, levels * lats))
    grid = lax.dot_general(
        returned.reshape(devices * 2 * slots, levels, lats),
        table,
        (((0,), (0,)), ((), ())),
        precision=PRECISION,
        preferred_element_type=jnp.float32,
    )
    return spectral.transpose(0, 3, 1, 2), jnp.swapaxes(grid, 0, 1)


def solution(mesh):
    return jax.shard_map(
        shards,
        mesh=mesh,
        in_specs=(
            P("band", "lev", None),
            P("band", "lev", None),
            P(("band", "lev"), None, None),
            P(),
            P(("band", "lev"), None, None, None),
            P(),
            P(),
            P(),
        ),
        out_specs=(P(("band", "lev"), None, None, None), P("band", "lev", None)),
        check_vma=False,
    )
```
